32 devices in a mesh: dp: 2 (over y), tensor: 16 (over z, x, core).
Axes of the slice: x: 2, y: 2, z: 4, core: 2. Of those that a mesh axis runs over, the one named last changes fastest.
Arguments:
- inputs: float32 [256, 4096], P('dp', 'tensor'), may hold values from -6 to 6
- out_grad: float32 [256, 4096], P('dp', 'tensor'), may hold values from -6 to 6
- up_weight: float32 [768, 128, 128], P('tensor'), may hold values from -0.25 to 0.25
- down_weight: float32 [768, 128, 128], P('tensor'), may hold values from -0.109375 to 0.109375
- up_left: float32 [4096, 128], P('tensor'), may hold values from -0.09375 to 0.09375
- up_right: float32 [128, 16384], P(None, 'tensor'), may hold values from -0.5 to 0.5
- down_left: float32 [16384, 128], P('tensor'), may hold values from -0.046875 to 0.046875
- down_right: float32 [128, 4096], P(None, 'tensor'), may hold values from -0.5 to 0.5
- model_block: int32 [768], P('tensor'), may hold values from 0 to 31, as said below
- hidden_block: int32 [768], P('tensor'), may hold values from 0 to 7
- live_slots: int32 [16], P('tensor'), may hold values from 24 to 48, as said below
Outputs:
- result: float32 [256, 4096], P('dp', 'tensor')
- input_grad: float32 [256, 4096], P('dp', 'tensor')
- up_grad: float32 [768, 128, 128], P('tensor', 'dp')
- down_grad: float32 [768, 128, 128], P('tensor', 'dp')
- up_left_grad: float32 [4096, 128], P(('tensor', 'dp'))
- up_right_grad: float32 [128, 16384], P('dp', 'tensor')
- down_left_grad: float32 [16384, 128], P(('tensor', 'dp'))
- down_right_grad: float32 [128, 4096], P('dp', 'tensor')
The draws below stay inside these ranges and needn't reach their ends.
Inputs may be any that keep to these rules, and one draw needn't show every extreme that they name: `model_block`: with g the slot's hidden block counted over all owners, the slot's model block differs from g mod 32 in at most one bit. `live_slots`: at least one owner has all 48 slots live.
All inputs are finite; a program needn't handle non-finite values.
Results may differ from the reference program's by a relative error of at most 0.0003.
Values sent between devices are 32-bit elements; how exact they have to be, the bound alone decides.
A program may use at most 64 MiB of HBM per device.

```python
import jax
import jax.numpy as jnp
from jax import lax

D = 4096
FF = 16384
BLK = 128
RANK = 128
TOKENS = 256
DBLOCKS = 32
HBLOCKS = 8
CAP = 48
OWNERS = 16
SLOTS = 768


def slot_pattern(key):
    folded = jax.random.fold_in(key, 7)
    key_hidden, key_level = jax.random.split(folded)
    hidden = jax.random.randint(key_hidden, (SLOTS,), 0, HBLOCKS, dtype=jnp.int32)
    levels = DBLOCKS.bit_length() - 1
    section_bit = jax.random.randint(key_level, (SLOTS,), 0, levels + 1, dtype=jnp.int32)
    owner_id = jnp.arange(SLOTS, dtype=jnp.int32) // CAP
    column = (owner_id * HBLOCKS + hidden) % DBLOCKS
    toggled = jnp.where(section_bit == levels, jnp.int32(0), jnp.left_shift(jnp.int32(1), jnp.minimum(section_bit, levels - 1)))
    return (hidden, jnp.bitwise_xor(column, toggled))


def draw_model_block(key, part):
    return slot_pattern(key)[1]


def draw_hidden_block(key, part):
    return slot_pattern(key)[0]


def draw_live_slots(key, part):
    folded = jax.random.fold_in(key, 13)
    key_count, key_full = jax.random.split(folded)
    counted = jax.random.randint(key_count, (OWNERS,), CAP // 2, CAP + 1, dtype=jnp.int32)
    full_owner = jax.random.randint(key_full, (), 0, OWNERS, dtype=jnp.int32)
    return jnp.where(jnp.arange(OWNERS, dtype=jnp.int32) == full_owner, jnp.int32(CAP), counted)


def level_of(stream_key, shape, cuts, least, top_value):
    def one(axis_at, blocks):
        draws = jax.random.uniform(jax.random.fold_in(jax.random.fold_in(stream_key, 6), axis_at), (blocks,), jnp.float32, least / len(cuts), top_value / len(cuts))
        return jnp.repeat(jnp.exp(draws), shape[axis_at] // blocks).reshape((-1,) + (1,) * (len(shape) - axis_at - 1))

    level = one(*cuts[0])
    for cut in cuts[1:]:
        level = level * one(*cut)
    return level


def gaussian(rng, shape, width, reach, cuts=(), kind=jnp.bfloat16):
    loudness = level_of(rng, shape, cuts, -0.22, 0.18) if cuts else 1.0
    array = jax.random.normal(rng, shape, jnp.float32) * width * loudness
    return jnp.minimum(jnp.maximum(array, -reach), reach).astype(kind)


def setup_inputs(seed: int = 0) -> dict:
    key_of = jax.random.split(jax.random.key(seed), 12)
    return {
        "inputs": gaussian(key_of[0], (TOKENS, D), 1.0, 6.0, ((0, 2), (1, 16)), jnp.float32),
        "out_grad": gaussian(key_of[1], (TOKENS, D), 1.0, 6.0, ((0, 2), (1, 16)), jnp.float32),
        "up_weight": gaussian(key_of[2], (SLOTS, BLK, BLK), (5 * BLK) ** -0.5, 0.25, ((0, 16),), jnp.float32),
        "down_weight": gaussian(key_of[3], (SLOTS, BLK, BLK), (SLOTS * BLK // DBLOCKS) ** -0.5, 0.109375, ((0, 16),), jnp.float32),
        "up_left": gaussian(key_of[4], (D, RANK), D ** -0.5, 0.09375, ((0, 16),), jnp.float32),
        "up_right": gaussian(key_of[5], (RANK, FF), RANK ** -0.5, 0.5, ((1, 16),), jnp.float32),
        "down_left": gaussian(key_of[6], (FF, RANK), FF ** -0.5, 0.046875, ((0, 16),), jnp.float32),
        "down_right": gaussian(key_of[7], (RANK, D), RANK ** -0.5, 0.5, ((1, 16),), jnp.float32),
        "model_block": draw_model_block(jax.random.fold_in(key_of[11], 71), 0),
        "hidden_block": draw_hidden_block(jax.random.fold_in(key_of[11], 71), 0),
        "live_slots": draw_live_slots(jax.random.fold_in(key_of[11], 71), 0),
    }


highest = lax.Precision.HIGHEST

def activation(values):
    return jax.nn.gelu(values, approximate=True)

def onehot(indices, extent):
    return (indices[:, None] == jnp.arange(extent, dtype=jnp.int32)[None, :]).astype(jnp.float32)

def reference(inputs, out_grad, up_weight, down_weight, up_left, up_right, down_left, down_right, model_block, hidden_block, live_slots):
    row_count = inputs.shape[0]
    hidden_width = HBLOCKS * BLK
    slot_index = jnp.arange(SLOTS, dtype=jnp.int32)
    owner_id = slot_index // CAP
    alive_mask = (slot_index % CAP < live_slots[owner_id]).astype(jnp.float32)
    up_live = (up_weight * alive_mask[:, None, None]).reshape(OWNERS, CAP, BLK, BLK)
    down_live = (down_weight * alive_mask[:, None, None]).reshape(OWNERS, CAP, BLK, BLK)
    model_owned = model_block.reshape(OWNERS, CAP)
    hidden_owned = hidden_block.reshape(OWNERS, CAP)
    alive_owned = alive_mask.reshape(OWNERS, CAP)
    right_owned = up_right.reshape(RANK, OWNERS, hidden_width).transpose(1, 0, 2)
    left_owned = down_left.reshape(OWNERS, hidden_width, RANK)
    split_in = inputs.reshape(row_count, DBLOCKS, BLK)
    split_grad = out_grad.reshape(row_count, DBLOCKS, BLK)
    low_in = jnp.dot(inputs, up_left, precision=highest)

    def forward_up(running, pieces):
        weight, models, hiddens, right = pieces
        chosen = jnp.take(split_in, models, axis=1)
        slot_out = jnp.einsum('tsk,skn->tsn', chosen, weight, precision=highest)
        merged = jnp.einsum('tsn,sh->thn', slot_out, onehot(hiddens, HBLOCKS), precision=highest)
        return (running, merged.reshape(row_count, hidden_width) + jnp.dot(low_in, right, precision=highest))
    _, preact = lax.scan(forward_up, jnp.zeros((), jnp.float32), (up_live, model_owned, hidden_owned, right_owned))
    hidden = activation(preact)
    low_mid = jnp.einsum('otw,owr->tr', hidden, left_owned, precision=highest)

    def forward_down(running, pieces):
        weight, models, hiddens, hidden_part = pieces
        chosen = jnp.take(hidden_part.reshape(row_count, HBLOCKS, BLK), hiddens, axis=1)
        slot_out = jnp.einsum('tsk,skn->tsn', chosen, weight, precision=highest)
        placed = jnp.einsum('tsn,sm->tmn', slot_out, onehot(models, DBLOCKS), precision=highest)
        return (running + placed.reshape(row_count, D), jnp.zeros((), jnp.float32))
    sparse_out, _ = lax.scan(forward_down, jnp.zeros((row_count, D), jnp.float32), (down_live, model_owned, hidden_owned, hidden))
    result = sparse_out + jnp.dot(low_mid, down_right, precision=highest)
    back_mid = jnp.dot(out_grad, down_right.T, precision=highest)

    def backward_down(running, pieces):
        weight, models, hiddens, alive, hidden_part, preact_part, left = pieces
        chosen_grad = jnp.take(split_grad, models, axis=1)
        slot_back = jnp.einsum('tsn,skn->tsk', chosen_grad, weight, precision=highest)
        merged = jnp.einsum('tsk,sh->thk', slot_back, onehot(hiddens, HBLOCKS), precision=highest)
        hidden_grad = merged.reshape(row_count, hidden_width) + jnp.dot(back_mid, left.T, precision=highest)
        _, pullback = jax.vjp(activation, preact_part)
        preact_grad = pullback(hidden_grad)[0]
        chosen_hidden = jnp.take(hidden_part.reshape(row_count, HBLOCKS, BLK), hiddens, axis=1)
        weight_grad = jnp.einsum('tsk,tsn->skn', chosen_hidden, chosen_grad, precision=highest) * alive[:, None, None]
        left_grad = jnp.dot(hidden_part.T, back_mid, precision=highest)
        return (running, (preact_grad, weight_grad, left_grad))
    _, (preact_grad, down_grad, down_left_grad) = lax.scan(backward_down, jnp.zeros((), jnp.float32), (down_live, model_owned, hidden_owned, alive_owned, hidden, preact, left_owned))
    back_in = jnp.einsum('otw,orw->tr', preact_grad, right_owned, precision=highest)

    def backward_up(running, pieces):
        weight, models, hiddens, alive, grad_part = pieces
        chosen_grad = jnp.take(grad_part.reshape(row_count, HBLOCKS, BLK), hiddens, axis=1)
        slot_back = jnp.einsum('tsn,skn->tsk', chosen_grad, weight, precision=highest)
        placed = jnp.einsum('tsk,sm->tmk', slot_back, onehot(models, DBLOCKS), precision=highest)
        chosen_in = jnp.take(split_in, models, axis=1)
        weight_grad = jnp.einsum('tsk,tsn->skn', chosen_in, chosen_grad, precision=highest) * alive[:, None, None]
        return (running + placed.reshape(row_count, D), weight_grad)
    sparse_in, up_grad = lax.scan(backward_up, jnp.zeros((row_count, D), jnp.float32), (up_live, model_owned, hidden_owned, alive_owned, preact_grad))
    input_grad = sparse_in + jnp.dot(back_in, up_left.T, precision=highest)
    up_left_grad = jnp.dot(inputs.T, back_in, precision=highest)
    up_right_grad = jnp.einsum('tr,otw->row', low_in, preact_grad, precision=highest).reshape(RANK, FF)
    down_right_grad = jnp.dot(low_mid.T, out_grad, precision=highest)
    return (result, input_grad, up_grad.reshape(SLOTS, BLK, BLK), down_grad.reshape(SLOTS, BLK, BLK), up_left_grad, up_right_grad, down_left_grad.reshape(FF, RANK), down_right_grad)
```

```python
import functools

import jax
import jax.numpy as jnp
from jax import lax
from jax.experimental import pallas as pl
from jax.experimental.pallas import tpu as pltpu
from jax.sharding import PartitionSpec as P

MESH = pl.DeviceIdType.MESH
VM = pl.BlockSpec(memory_space=pltpu.VMEM)
SM = pl.BlockSpec(memory_space=pltpu.SMEM)
f32 = jnp.float32


def halves(v):
    hi = v.astype(jnp.bfloat16)
    lo = (v - hi.astype(f32)).astype(jnp.bfloat16)
    return hi, lo


def left3(v, axis):
    hi, lo = halves(v)
    return jnp.concatenate([hi, hi, lo], axis=axis)


def right3(v, axis):
    hi, lo = halves(v)
    return jnp.concatenate([hi, lo, hi], axis=axis)


def contract(a, b, da, db):
    return lax.dot_general(a, b, (((da,), (db,)), ((), ())), preferred_element_type=f32)


def dot3(a, b, da, db):
    return contract(left3(a, da), right3(b, db), da, db)


def flip(a, k, size):
    out, bit = 0, 1
    while bit < size:
        out = out + (((a // bit) % 2 + (k // bit) % 2) % 2) * bit
        bit *= 2
    return out


class Copies:
    def __init__(self, sems):
        self.sems, self.count, self.made = sems, 0, []

    def send(self, src, dst, recv, where, cond=None):
        sem = self.sems.at[self.count]
        self.count += 1
        copy = pltpu.make_async_remote_copy(
            src_ref=src, dst_ref=dst, send_sem=sem, recv_sem=recv, device_id=where, device_id_type=MESH
        )
        if cond is None:
            copy.start()
        else:
            pl.when(cond)(copy.start)
        self.made.append((copy, cond))

    def drain(self):
        for copy, cond in self.made:
            if cond is None:
                copy.wait_send()
            else:
                pl.when(cond)(copy.wait_send)


def arrived(ref, recv, where):
    pltpu.make_async_remote_copy(
        src_ref=ref, dst_ref=ref, send_sem=recv, recv_sem=recv, device_id=where, device_id_type=MESH
    ).wait_recv()


def greet(d, t, dp, T):
    barrier = pltpu.get_barrier_semaphore()
    for k in range(1, T):
        pl.semaphore_signal(barrier, inc=1, device_id=(d, lax.rem(t + k, T)), device_id_type=MESH)
    for k in range(1, dp):
        pl.semaphore_signal(barrier, inc=1, device_id=(lax.rem(d + k, dp), t), device_id_type=MESH)
    pl.semaphore_wait(barrier, T - 1 + dp - 1)


class Total:
    def __init__(self, out, d, t, T, part, inbox, copies, in_sem, out_sem):
        self.out, self.d, self.t, self.T, self.part, self.inbox = out, d, t, T, part, inbox
        self.copies, self.in_sem, self.out_sem = copies, in_sem, out_sem
        rank = part.shape[1]
        self.rows = max(8, rank // T)
        self.count = rank // self.rows

    def cond(self, j):
        return None if self.count >= self.T else j < self.count

    def piece(self, ref, j):
        return ref.at[:, pl.ds(pl.multiple_of(j * self.rows, self.rows), self.rows), :]

    def begin(self):
        for k in range(1, self.T):
            j = lax.rem(self.t + k, self.T)
            cond = self.cond(j)
            at = j if cond is None else lax.rem(j, self.count)
            self.copies.send(
                self.piece(self.part, at), self.inbox.at[self.T - k], self.in_sem.at[self.T - k], (self.d, j), cond
            )

    def reduce(self):
        cond = self.cond(self.t)
        at = self.t if cond is None else lax.rem(self.t, self.count)

        def work():
            span = pl.ds(pl.multiple_of(at * self.rows, self.rows), self.rows)
            total = self.part[:, span, :]
            for k in range(1, self.T):
                arrived(self.inbox.at[k], self.in_sem.at[k], (self.d, self.t))
                total = total + self.inbox[k]
            self.out[:, span, :] = total

        if cond is None:
            work()
        else:
            pl.when(cond)(work)
        for k in range(1, self.T):
            j = lax.rem(self.t + k, self.T)
            self.copies.send(
                self.piece(self.out, at), self.piece(self.out, at), self.out_sem.at[self.T - k], (self.d, j), cond
            )

    def finish(self):
        for k in range(1, self.T):
            j = lax.rem(self.t + k, self.T)
            cond = self.cond(j)
            at = j if cond is None else lax.rem(j, self.count)
            wait = functools.partial(arrived, self.piece(self.out, at), self.out_sem.at[k], (self.d, j))
            if cond is None:
                wait()
            else:
                pl.when(cond)(wait)


def gather_kernel(
    dp, T, x_ref, g_ref, upl_ref, dnr_ref,
    full, peer_g, peer_x, peer_own, red, peer_red,
    part, inbox, send_sem, full_sem, pg_sem, px_sem, po_sem, in_sem, out_sem, pr_sem,
):
    d, t = lax.axis_index("dp"), lax.axis_index("tensor")
    c, b, a = t % 2, (t // 2) % 2, t // 4
    A = T // 4
    bps, blk = x_ref.shape[0], x_ref.shape[1]
    part_rows = blk // dp
    core, side = (d, a * 4 + b * 2 + 1 - c), (d, a * 4 + (1 - b) * 2 + c)
    copies = Copies(send_sem)
    greet(d, t, dp, T)

    def to_peers(src_x, src_g, s):
        for k in range(dp - 1):
            other = lax.rem(d + k + 1, dp)
            rows = pl.ds(pl.multiple_of(other * part_rows, part_rows), part_rows)
            copies.send(src_g, peer_g.at[k, s], pg_sem.at[k, s], (other, t))
            copies.send(src_x.at[:, rows, :], peer_x.at[k, s], px_sem.at[k, s], (other, t))

    def two(src_x, src_g, s, where):
        copies.send(src_x, full.at[s, 0], full_sem.at[s, 0], where)
        copies.send(src_g, full.at[s, 1], full_sem.at[s, 1], where)

    def got(s, where):
        arrived(full.at[s, 0], full_sem.at[s, 0], where)
        arrived(full.at[s, 1], full_sem.at[s, 1], where)

    for k in range(1, A):
        two(x_ref, g_ref, t, (d, flip(a, k, A) * 4 + b * 2 + c))
    two(x_ref, g_ref, t, side)
    two(x_ref, g_ref, t, core)
    to_peers(x_ref, g_ref, t)
    for k in range(dp - 1):
        copies.send(x_ref, peer_own.at[k], po_sem.at[k], (lax.rem(d + k + 1, dp), t))
    feats = bps * blk
    part[0] = dot3(upl_ref[...], x_ref[...].reshape(feats, x_ref.shape[2]), 0, 0)
    part[1] = dot3(dnr_ref[...], g_ref[...].reshape(feats, x_ref.shape[2]), 1, 0)
    total = Total(red, d, t, T, part, inbox, copies, in_sem, out_sem)
    total.begin()
    full[t, 0] = x_ref[...]
    full[t, 1] = g_ref[...]
    total.reduce()
    mine = []
    for k in range(A):
        row = flip(a, k, A)
        s = row * 4 + b * 2 + c
        if k > 0:
            got(s, side)
            two(full.at[s, 0], full.at[s, 1], s, side)
            two(full.at[s, 0], full.at[s, 1], s, core)
            to_peers(full.at[s, 0], full.at[s, 1], s)
        mine.append(s)
        s = row * 4 + (1 - b) * 2 + c
        got(s, side)
        two(full.at[s, 0], full.at[s, 1], s, core)
        to_peers(full.at[s, 0], full.at[s, 1], s)
        mine.append(s)
    total.finish()
    for k in range(dp - 1):
        copies.send(red, peer_red.at[k], pr_sem.at[k], (lax.rem(d + k + 1, dp), t))
    for s in mine:
        for k in range(dp - 1):
            arrived(peer_g.at[k, s], pg_sem.at[k, s], core)
            arrived(peer_x.at[k, s], px_sem.at[k, s], core)
            copies.send(peer_g.at[k, s], peer_g.at[k, s], pg_sem.at[k, s], core)
            copies.send(peer_x.at[k, s], peer_x.at[k, s], px_sem.at[k, s], core)
    for k in range(2 * A):
        s = k * 2 + 1 - c
        got(s, core)
        for p in range(dp - 1):
            arrived(peer_g.at[p, s], pg_sem.at[p, s], core)
            arrived(peer_x.at[p, s], px_sem.at[p, s], core)
    for k in range(dp - 1):
        arrived(peer_own.at[k], po_sem.at[k], core)
        arrived(peer_red.at[k], pr_sem.at[k], core)
    copies.drain()


def scatter_kernel(
    dp, T, terms, low, hd,
    summed, red, peer_hd, peer_red,
    core_box, stage, side_box, acc, line_box, inbox,
    send_sem, core_sem, side_sem, line_sem, hd_sem, in_sem, out_sem, pr_sem,
):
    d, t = lax.axis_index("dp"), lax.axis_index("tensor")
    c, b, a = t % 2, (t // 2) % 2, t // 4
    A = T // 4
    core, side = (d, a * 4 + b * 2 + 1 - c), (d, a * 4 + (1 - b) * 2 + c)
    copies = Copies(send_sem)
    greet(d, t, dp, T)
    order = [flip(a, k, A) for k in range(A)][::-1]
    for far in (1, 0):
        for row in order:
            col = (1 - b) if far else b
            i = row * 2 + col
            copies.send(terms.at[i * 2 + 1 - c], core_box.at[i], core_sem.at[i], core)
    for k in range(dp - 1):
        for n in range(2):
            copies.send(hd.at[n], peer_hd.at[k, n], hd_sem.at[k, n], (lax.rem(d + k + 1, dp), t))
    total = Total(red, d, t, T, low, inbox, copies, in_sem, out_sem)
    total.begin()
    for row in order:
        i = row * 2 + 1 - b
        arrived(core_box.at[i], core_sem.at[i], core)
        stage[row] = terms[i * 2 + c] + core_box[i]
        copies.send(stage.at[row], side_box.at[row], side_sem.at[row], side)
    total.reduce()
    for n, row in enumerate(order):
        i = row * 2 + b
        k = A - 1 - n
        arrived(core_box.at[i], core_sem.at[i], core)
        arrived(side_box.at[row], side_sem.at[row], side)
        acc[row] = terms[i * 2 + c] + core_box[i] + side_box[row]
        if k > 0:
            copies.send(acc.at[row], line_box.at[k], line_sem.at[k], (d, row * 4 + b * 2 + c))
    total.finish()
    for k in range(dp - 1):
        copies.send(red, peer_red.at[k], pr_sem.at[k], (lax.rem(d + k + 1, dp), t))
    result = acc[a]
    for k in range(1, A):
        arrived(line_box.at[k], line_sem.at[k], core)
        result = result + line_box[k]
    summed[...] = result
    for k in range(dp - 1):
        arrived(peer_hd.at[k, 0], hd_sem.at[k, 0], core)
        arrived(peer_hd.at[k, 1], hd_sem.at[k, 1], core)
        arrived(peer_red.at[k], pr_sem.at[k], core)
    copies.drain()


def layer_kernel(
    unroll, mb_ref, hb_ref, live_ref, full, red, upw, dnw, upr, dnl,
    terms, low, hd,
    split_x, split_g, split_hd, pre, grad,
):
    slots, blk = upw.shape[0], upw.shape[1]
    bps, tokens = full.shape[2], full.shape[4]
    blocks = hd.shape[1]
    live = live_ref[0]

    @pl.loop(0, full.shape[0])
    def _(s):
        for j in range(bps):
            split_x[s * bps + j] = right3(full[s, 0, j], 0)
            split_g[s * bps + j] = right3(full[s, 1, j], 0)
            terms[s, 0, j] = jnp.zeros((blk, tokens), f32)
            terms[s, 1, j] = jnp.zeros((blk, tokens), f32)

    low_in, back_mid = right3(red[0], 0), right3(red[1], 0)
    for h in range(blocks):
        pre[h] = contract(left3(upr[:, h * blk : (h + 1) * blk], 0), low_in, 0, 0)
        grad[h] = contract(left3(dnl[h * blk : (h + 1) * blk, :], 1), back_mid, 1, 0)

    @pl.loop(0, pl.cdiv(live, unroll))
    def _(i):
        done = []
        for j in range(unroll):
            s = i * unroll + j
            keep = (s < live).astype(f32)
            m = mb_ref[s]
            up = contract(left3(upw[s] * keep, 0), split_x[m], 0, 0)
            dn = contract(left3(dnw[s] * keep, 1), split_g[m], 1, 0)
            done.append((hb_ref[s], up, dn))
        for h, up, dn in done:
            pre[h] += up
            grad[h] += dn

    scale = 0.7978845608028654
    for h in range(blocks):
        v = pre[h]
        th = jnp.tanh(scale * (v + 0.044715 * (v * v * v)))
        hidden = 0.5 * v * (1.0 + th)
        slope = 0.5 * (1.0 + th) + 0.5 * v * (1.0 - th * th) * (scale * (1.0 + 3 * 0.044715 * (v * v)))
        back = grad[h] * slope
        hd[0, h] = hidden
        hd[1, h] = back
        hs, bs = right3(hidden, 0), right3(back, 0)
        split_hd[0, h] = hs
        split_hd[1, h] = bs
        lm = contract(left3(dnl[h * blk : (h + 1) * blk, :], 0), hs, 0, 0)
        bi = contract(left3(upr[:, h * blk : (h + 1) * blk], 1), bs, 1, 0)
        if h == 0:
            low[0] = lm
            low[1] = bi
        else:
            low[0] += lm
            low[1] += bi

    @pl.loop(0, pl.cdiv(live, unroll))
    def _(i):
        done = []
        for j in range(unroll):
            s = i * unroll + j
            keep = (s < live).astype(f32)
            h = hb_ref[s]
            dn = contract(left3(dnw[s] * keep, 0), split_hd[0, h], 0, 0)
            up = contract(left3(upw[s] * keep, 1), split_hd[1, h], 1, 0)
            done.append((mb_ref[s], dn, up))
        for m, dn, up in done:
            terms[m // bps, 0, m % bps] += dn
            terms[m // bps, 1, m % bps] += up


def grads_kernel(
    dp, unroll, mb_ref, hb_ref, live_ref,
    full, peer_g, peer_x, hd, peer_hd,
    x_ref, g_ref, peer_own, peer_own_g, red, peer_red, low, peer_low, summed, upl, dnr,
    res, ing, upg, dng, uplg, uprg, dnlg, dnrg,
):
    slots, rows, blk = upg.shape
    bps = full.shape[2]
    blocks = hd.shape[1]
    d = lax.axis_index("dp")
    live = live_ref[0]
    mine = pl.ds(pl.multiple_of(d * rows, rows), rows)
    peers = range(dp - 1)

    def cat(first, rest):
        return jnp.concatenate([first] + rest, axis=1)

    @pl.loop(0, slots // unroll)
    def _(i):
        for j in range(unroll):
            s = i * unroll + j
            keep = (s < live).astype(f32)
            m, h = mb_ref[s], hb_ref[s]
            q, r = m // bps, m % bps
            x = cat(full[q, 0, r, mine, :], [peer_x[k, q, r] for k in peers])
            back = cat(hd[1, h], [peer_hd[k, 1, h] for k in peers])
            upg[s] = dot3(x, back, 1, 1) * keep
            hidden = cat(hd[0, h, mine, :], [peer_hd[k, 0, h, mine, :] for k in peers])
            g = cat(full[q, 1, r], [peer_g[k, q, r] for k in peers])
            dng[s] = dot3(hidden, g, 1, 1) * keep

    res[...] = summed[0].reshape(bps * blk, -1) + dot3(dnr[...], low[0], 0, 0)
    ing[...] = summed[1].reshape(bps * blk, -1) + dot3(upl[...], low[1], 1, 0)
    n = uplg.shape[0]
    span = pl.ds(pl.multiple_of(d * n, n), n)
    x = cat(x_ref[span, :], [peer_own[k, span, :] for k in peers])
    uplg[...] = dot3(x, cat(low[1], [peer_low[k, 1] for k in peers]), 1, 1)
    n = uprg.shape[0]
    span = pl.ds(pl.multiple_of(d * n, n), n)
    left_in = left3(cat(red[0, span, :], [peer_red[k, 0, span, :] for k in peers]), 1)
    left_mid = left3(cat(low[0, span, :], [peer_low[k, 0, span, :] for k in peers]), 1)
    for h in range(blocks):
        back = cat(hd[1, h], [peer_hd[k, 1, h] for k in peers])
        uprg[:, h * blk : (h + 1) * blk] = contract(left_in, right3(back, 1), 1, 1)
    g = cat(g_ref[...], [peer_own_g[k] for k in peers])
    dnrg[...] = contract(left_mid, right3(g, 1), 1, 1)
    back_mid = right3(cat(red[1], [peer_red[k, 1] for k in peers]), 1)
    n = dnlg.shape[0]
    step = min(n, blk)
    for j in range(n // step):
        at = d * n + j * step
        h = at // blk
        inner = pl.ds(pl.multiple_of(at % blk, step), step)
        hidden = cat(hd[0, h, inner, :], [peer_hd[k, 0, h, inner, :] for k in peers])
        dnlg[j * step : (j + 1) * step, :] = contract(left3(hidden, 1), back_mid, 1, 1)


def shards(
    dp, T,
    inputs, out_grad, up_weight, down_weight, up_left, up_right, down_left, down_right,
    model_block, hidden_block, live_slots,
):
    tokens, feats = inputs.shape
    slots, blk = up_weight.shape[0], up_weight.shape[1]
    width = up_right.shape[1]
    rank = up_left.shape[1]
    blocks = width // blk
    bps = feats // blk
    A = T // 4
    peers = dp - 1
    unroll = 4 if slots % 4 == 0 else 1
    DMA = pltpu.SemaphoreType.DMA
    sds = lambda *shape: jax.ShapeDtypeStruct(shape, f32)
    sends = 2 * (A - 1) + 2 * A + 4 * A + peers * (8 * A + 2) + 2 * (T - 1)
    rows = max(8, rank // T)
    limit = 60 << 20
    x_t = inputs.T.reshape(bps, blk, tokens)
    g_t = out_grad.T.reshape(bps, blk, tokens)
    full, peer_g, peer_x, peer_own, red, peer_red = pl.pallas_call(
        functools.partial(gather_kernel, dp, T),
        out_shape=(
            sds(T, 2, bps, blk, tokens),
            sds(peers, T, bps, blk, tokens),
            sds(peers, T, bps, blk // dp, tokens),
            sds(peers, bps, blk, tokens),
            sds(2, rank, tokens),
            sds(peers, 2, rank, tokens),
        ),
        in_specs=[VM] * 4,
        out_specs=[VM] * 6,
        scratch_shapes=[
            pltpu.VMEM((2, rank, tokens), f32),
            pltpu.VMEM((T, 2, rows, tokens), f32),
            DMA((sends,)), DMA((T, 2)), DMA((peers, T)), DMA((peers, T)), DMA((peers,)),
            DMA((T,)), DMA((T,)), DMA((peers,)),
        ],
        compiler_params=pltpu.CompilerParams(collective_id=0, has_side_effects=True, vmem_limit_bytes=limit),
    )(x_t, g_t, up_left, down_right)
    terms, low, hd = pl.pallas_call(
        functools.partial(layer_kernel, unroll),
        out_shape=(
            sds(T, 2, bps, blk, tokens),
            sds(2, rank, tokens),
            sds(2, blocks, blk, tokens),
        ),
        in_specs=[SM] * 3 + [VM] * 6,
        out_specs=[VM] * 3,
        scratch_shapes=[
            pltpu.VMEM((T * bps, 3 * blk, tokens), jnp.bfloat16),
            pltpu.VMEM((T * bps, 3 * blk, tokens), jnp.bfloat16),
            pltpu.VMEM((2, blocks, 3 * blk, tokens), jnp.bfloat16),
            pltpu.VMEM((blocks, blk, tokens), f32),
            pltpu.VMEM((blocks, blk, tokens), f32),
        ],
        compiler_params=pltpu.CompilerParams(vmem_limit_bytes=limit),
    )(model_block, hidden_block, live_slots, full, red, up_weight, down_weight, up_right, down_left)
    sends = 2 * A + A + (A - 1) + peers * 3 + 2 * (T - 1)
    summed, low_total, peer_hd, peer_low = pl.pallas_call(
        functools.partial(scatter_kernel, dp, T),
        out_shape=(
            sds(2, bps, blk, tokens),
            sds(2, rank, tokens),
            sds(peers, 2, blocks, blk, tokens),
            sds(peers, 2, rank, tokens),
        ),
        in_specs=[VM] * 3,
        out_specs=[VM] * 4,
        scratch_shapes=[
            pltpu.VMEM((2 * A, 2, bps, blk, tokens), f32),
            pltpu.VMEM((A, 2, bps, blk, tokens), f32),
            pltpu.VMEM((A, 2, bps, blk, tokens), f32),
            pltpu.VMEM((A, 2, bps, blk, tokens), f32),
            pltpu.VMEM((A, 2, bps, blk, tokens), f32),
            pltpu.VMEM((T, 2, rows, tokens), f32),
            DMA((sends,)), DMA((2 * A,)), DMA((A,)), DMA((A,)), DMA((peers, 2)),
            DMA((T,)), DMA((T,)), DMA((peers,)),
        ],
        compiler_params=pltpu.CompilerParams(collective_id=1, has_side_effects=True, vmem_limit_bytes=limit),
    )(terms, low, hd)
    own = lax.axis_index("tensor")
    peer_own_g = lax.dynamic_index_in_dim(peer_g, own, 1, keepdims=False).reshape(peers, feats, tokens)
    res, ing, upg, dng, uplg, uprg, dnlg, dnrg = pl.pallas_call(
        functools.partial(grads_kernel, dp, unroll),
        out_shape=(
            sds(feats, tokens),
            sds(feats, tokens),
            sds(slots, blk // dp, blk),
            sds(slots, blk // dp, blk),
            sds(feats // dp, rank),
            sds(rank // dp, width),
            sds(width // dp, rank),
            sds(rank // dp, feats),
        ),
        in_specs=[SM] * 3 + [VM] * 16,
        out_specs=[VM] * 8,
        compiler_params=pltpu.CompilerParams(vmem_limit_bytes=limit),
    )(
        model_block, hidden_block, live_slots,
        full, peer_g, peer_x, hd, peer_hd,
        x_t.reshape(feats, tokens), g_t.reshape(feats, tokens),
        peer_own.reshape(peers, feats, tokens), peer_own_g,
        red, peer_red, low_total, peer_low, summed, up_left, down_right,
    )
    return res.T, ing.T, upg, dng, uplg, uprg, dnlg, dnrg


def solution(mesh):
    return jax.shard_map(
        functools.partial(shards, mesh.shape["dp"], mesh.shape["tensor"]),
        mesh=mesh,
        in_specs=(
            P("dp", "tensor"),
            P("dp", "tensor"),
            P("tensor", None, None),
            P("tensor", None, None),
            P("tensor", None),
            P(None, "tensor"),
            P("tensor", None),
            P(None, "tensor"),
            P("tensor"),
            P("tensor"),
            P("tensor"),
        ),
        out_specs=(
            P("dp", "tensor"),
            P("dp", "tensor"),
            P("tensor", "dp", None),
            P("tensor", "dp", None),
            P(("tensor", "dp"), None),
            P("dp", "tensor"),
            P(("tensor", "dp"), None),
            P("dp", "tensor"),
        ),
        check_vma=False,
    )
```

```python
import functools

import jax
import jax.numpy as jnp
from jax import lax
from jax.experimental import pallas as pl
from jax.experimental.pallas import tpu as pltpu
from jax.sharding import PartitionSpec as P

MESH = pl.DeviceIdType.MESH
VM = pl.BlockSpec(memory_space=pltpu.VMEM)
SM = pl.BlockSpec(memory_space=pltpu.SMEM)
f32 = jnp.float32


def halves(v):
    hi = v.astype(jnp.bfloat16)
    lo = (v - hi.astype(f32)).astype(jnp.bfloat16)
    return hi, lo


def left3(v, axis):
    hi, lo = halves(v)
    return jnp.concatenate([hi, hi, lo], axis=axis)


def right3(v, axis):
    hi, lo = halves(v)
    return jnp.concatenate([hi, lo, hi], axis=axis)


def contract(a, b, da, db):
    return lax.dot_general(a, b, (((da,), (db,)), ((), ())), preferred_element_type=f32)


def dot3(a, b, da, db):
    return contract(left3(a, da), right3(b, db), da, db)


def flip(a, k, size):
    out, bit = 0, 1
    while bit < size:
        out = out + (((a // bit) % 2 + (k // bit) % 2) % 2) * bit
        bit *= 2
    return out


class Copies:
    def __init__(self, sems):
        self.sems, self.count, self.made = sems, 0, []

    def send(self, src, dst, recv, where, cond=None):
        sem = self.sems.at[self.count]
        self.count += 1
        copy = pltpu.make_async_remote_copy(
            src_ref=src, dst_ref=dst, send_sem=sem, recv_sem=recv, device_id=where, device_id_type=MESH
        )
        if cond is None:
            copy.start()
        else:
            pl.when(cond)(copy.start)
        self.made.append((copy, cond))

    def drain(self):
        for copy, cond in self.made:
            if cond is None:
                copy.wait_send()
            else:
                pl.when(cond)(copy.wait_send)


def arrived(ref, recv, where, cond=None):
    copy = pltpu.make_async_remote_copy(
        src_ref=ref, dst_ref=ref, send_sem=recv, recv_sem=recv, device_id=where, device_id_type=MESH
    )
    if cond is None:
        copy.wait_recv()
    else:
        pl.when(cond)(copy.wait_recv)


def line_steps(a, A):
    out = [(a, 0, None)]
    for k in range(1, A):
        out.append(((a + A - k) % A, -1, a >= k))
        out.append(((a + k) % A, 1, a + k < A))
    return out


def greet(d, t, dp, T):
    barrier = pltpu.get_barrier_semaphore()
    for k in range(1, T):
        pl.semaphore_signal(barrier, inc=1, device_id=(d, lax.rem(t + k, T)), device_id_type=MESH)
    for k in range(1, dp):
        pl.semaphore_signal(barrier, inc=1, device_id=(lax.rem(d + k, dp), t), device_id_type=MESH)
    pl.semaphore_wait(barrier, T - 1 + dp - 1)


class Total:
    def __init__(self, out, d, t, T, part, inbox, copies, in_sem, out_sem):
        self.out, self.d, self.t, self.T, self.part, self.inbox = out, d, t, T, part, inbox
        self.copies, self.in_sem, self.out_sem = copies, in_sem, out_sem
        rank = part.shape[1]
        self.rows = max(8, rank // T)
        self.count = rank // self.rows

    def cond(self, j):
        return None if self.count >= self.T else j < self.count

    def piece(self, ref, j):
        return ref.at[:, pl.ds(pl.multiple_of(j * self.rows, self.rows), self.rows), :]

    def begin(self):
        for k in range(1, self.T):
            j = lax.rem(self.t + k, self.T)
            cond = self.cond(j)
            at = j if cond is None else lax.rem(j, self.count)
            self.copies.send(
                self.piece(self.part, at), self.inbox.at[self.T - k], self.in_sem.at[self.T - k], (self.d, j), cond
            )

    def reduce(self):
        cond = self.cond(self.t)
        at = self.t if cond is None else lax.rem(self.t, self.count)

        def work():
            span = pl.ds(pl.multiple_of(at * self.rows, self.rows), self.rows)
            total = self.part[:, span, :]
            for k in range(1, self.T):
                arrived(self.inbox.at[k], self.in_sem.at[k], (self.d, self.t))
                total = total + self.inbox[k]
            self.out[:, span, :] = total

        if cond is None:
            work()
        else:
            pl.when(cond)(work)
        for k in range(1, self.T):
            j = lax.rem(self.t + k, self.T)
            self.copies.send(
                self.piece(self.out, at), self.piece(self.out, at), self.out_sem.at[self.T - k], (self.d, j), cond
            )

    def finish(self):
        for k in range(1, self.T):
            j = lax.rem(self.t + k, self.T)
            cond = self.cond(j)
            at = j if cond is None else lax.rem(j, self.count)
            wait = functools.partial(arrived, self.piece(self.out, at), self.out_sem.at[k], (self.d, j))
            if cond is None:
                wait()
            else:
                pl.when(cond)(wait)


def gather_kernel(
    dp, T, inp_ref, og_ref, upl_ref, dnr_ref,
    full, peer_g, peer_own, red, peer_red,
    x_ref, g_ref, part, inbox, send_sem, full_sem, pg_sem, po_sem, in_sem, out_sem, pr_sem,
):
    d, t = lax.axis_index("dp"), lax.axis_index("tensor")
    c, b, a = t % 2, (t // 2) % 2, t // 4
    A = T // 4
    bps, blk = x_ref.shape[0], x_ref.shape[1]
    for j in range(bps):
        x_ref[j] = inp_ref[:, j * blk : (j + 1) * blk].T
        g_ref[j] = og_ref[:, j * blk : (j + 1) * blk].T
    core, side = (d, a * 4 + b * 2 + 1 - c), (d, a * 4 + (1 - b) * 2 + c)
    before, after = (d, (t + T - 4) % T), (d, (t + 4) % T)
    copies = Copies(send_sem)
    greet(d, t, dp, T)

    def to_peers(src_g, s, cond=None):
        for k in range(dp - 1):
            copies.send(src_g, peer_g.at[k, s], pg_sem.at[k, s], (lax.rem(d + k + 1, dp), t), cond)

    def two(src_x, src_g, s, where, cond=None):
        copies.send(src_x, full.at[s, 0], full_sem.at[s, 0], where, cond)
        copies.send(src_g, full.at[s, 1], full_sem.at[s, 1], where, cond)

    def got(s, where, cond=None):
        arrived(full.at[s, 0], full_sem.at[s, 0], where, cond)
        arrived(full.at[s, 1], full_sem.at[s, 1], where, cond)

    two(x_ref, g_ref, t, before, a >= 1)
    two(x_ref, g_ref, t, after, a + 1 < A)
    two(x_ref, g_ref, t, side)
    to_peers(g_ref, t)
    two(x_ref, g_ref, t, core)
    feats = bps * blk
    part[0] = dot3(upl_ref[...], x_ref[...].reshape(feats, x_ref.shape[2]), 0, 0)
    part[1] = dot3(dnr_ref[...], g_ref[...].reshape(feats, x_ref.shape[2]), 1, 0)
    total = Total(red, d, t, T, part, inbox, copies, in_sem, out_sem)
    total.begin()
    full[t, 0] = x_ref[...]
    full[t, 1] = g_ref[...]
    mine = []
    for row, way, here in line_steps(a, A):
        s = row * 4 + b * 2 + c
        if way != 0:
            got(s, side, here)
            onward = (here & (a + 1 < A)) if way < 0 else (here & (a >= 1))
            two(full.at[s, 0], full.at[s, 1], s, after if way < 0 else before, onward)
            two(full.at[s, 0], full.at[s, 1], s, side, here)
            to_peers(full.at[s, 1], s, here)
            two(full.at[s, 0], full.at[s, 1], s, core, here)
        mine.append((s, here))
        s = row * 4 + (1 - b) * 2 + c
        got(s, side, here)
        to_peers(full.at[s, 1], s, here)
        two(full.at[s, 0], full.at[s, 1], s, core, here)
        mine.append((s, here))
        if way == 0:
            total.reduce()
    total.finish()
    for k in range(dp - 1):
        copies.send(red, peer_red.at[k], pr_sem.at[k], (lax.rem(d + k + 1, dp), t))
        copies.send(x_ref, peer_own.at[k], po_sem.at[k], (lax.rem(d + k + 1, dp), t))
    for s, here in mine:
        for k in range(dp - 1):
            arrived(peer_g.at[k, s], pg_sem.at[k, s], core, here)
            copies.send(peer_g.at[k, s], peer_g.at[k, s], pg_sem.at[k, s], core, here)
    for k in range(2 * A):
        s = k * 2 + 1 - c
        got(s, core)
        for p in range(dp - 1):
            arrived(peer_g.at[p, s], pg_sem.at[p, s], core)
    for k in range(dp - 1):
        arrived(peer_own.at[k], po_sem.at[k], core)
        arrived(peer_red.at[k], pr_sem.at[k], core)
    copies.drain()


def scatter_kernel(
    dp, T, terms, low, hd, full,
    summed, red, peer_hd, peer_red, peer_x,
    core_box, stage, side_box, acc, line_box, inbox,
    send_sem, core_sem, side_sem, line_sem, hd_sem, px_sem, in_sem, out_sem, pr_sem,
):
    d, t = lax.axis_index("dp"), lax.axis_index("tensor")
    c, b, a = t % 2, (t // 2) % 2, t // 4
    A = T // 4
    core, side = (d, a * 4 + b * 2 + 1 - c), (d, a * 4 + (1 - b) * 2 + c)
    copies = Copies(send_sem)
    greet(d, t, dp, T)
    order = [flip(a, k, A) for k in range(A)][::-1]
    for far in (1, 0):
        for row in order:
            col = (1 - b) if far else b
            i = row * 2 + col
            copies.send(terms.at[i * 2 + 1 - c], core_box.at[i], core_sem.at[i], core)
    for k in range(dp - 1):
        for n in range(2):
            copies.send(hd.at[n], peer_hd.at[k, n], hd_sem.at[k, n], (lax.rem(d + k + 1, dp), t))
    total = Total(red, d, t, T, low, inbox, copies, in_sem, out_sem)
    total.begin()
    part_rows = peer_x.shape[3]
    for n in range(2 * A):
        for k in range(dp - 1):
            other = lax.rem(d + k + 1, dp)
            rows = pl.ds(pl.multiple_of(other * part_rows, part_rows), part_rows)
            s = n * 2 + c
            copies.send(full.at[s, 0, :, rows, :], peer_x.at[k, s], px_sem.at[k, s], (other, t))
    for row in order:
        i = row * 2 + 1 - b
        arrived(core_box.at[i], core_sem.at[i], core)
        stage[row] = terms[i * 2 + c] + core_box[i]
        copies.send(stage.at[row], side_box.at[row], side_sem.at[row], side)
    total.reduce()
    for n, row in enumerate(order):
        i = row * 2 + b
        k = A - 1 - n
        arrived(core_box.at[i], core_sem.at[i], core)
        arrived(side_box.at[row], side_sem.at[row], side)
        acc[row] = terms[i * 2 + c] + core_box[i] + side_box[row]
        if k > 0:
            copies.send(acc.at[row], line_box.at[k], line_sem.at[k], (d, row * 4 + b * 2 + c))
    total.finish()
    for k in range(dp - 1):
        copies.send(red, peer_red.at[k], pr_sem.at[k], (lax.rem(d + k + 1, dp), t))
    result = acc[a]
    for k in range(1, A):
        arrived(line_box.at[k], line_sem.at[k], core)
        result = result + line_box[k]
    summed[...] = result
    for n in range(2 * A):
        for k in range(dp - 1):
            s = n * 2 + c
            arrived(peer_x.at[k, s], px_sem.at[k, s], core)
            copies.send(peer_x.at[k, s], peer_x.at[k, s], px_sem.at[k, s], core)
    for k in range(dp - 1):
        arrived(peer_hd.at[k, 0], hd_sem.at[k, 0], core)
        arrived(peer_hd.at[k, 1], hd_sem.at[k, 1], core)
        for n in range(2 * A):
            s = n * 2 + 1 - c
            arrived(peer_x.at[k, s], px_sem.at[k, s], core)
        arrived(peer_red.at[k], pr_sem.at[k], core)
    copies.drain()


def layer_kernel(
    unroll, mb_ref, hb_ref, live_ref, full, red, upw, dnw, upr, dnl,
    terms, low, hd,
    split_x, split_g, split_hd, pre, grad,
):
    slots, blk = upw.shape[0], upw.shape[1]
    bps, tokens = full.shape[2], full.shape[4]
    blocks = hd.shape[1]
    live = live_ref[0]

    @pl.loop(0, full.shape[0])
    def _(s):
        for j in range(bps):
            split_x[s * bps + j] = right3(full[s, 0, j], 0)
            split_g[s * bps + j] = right3(full[s, 1, j], 0)
            terms[s, 0, j] = jnp.zeros((blk, tokens), f32)
            terms[s, 1, j] = jnp.zeros((blk, tokens), f32)

    low_in, back_mid = right3(red[0], 0), right3(red[1], 0)
    for h in range(blocks):
        pre[h] = contract(left3(upr[:, h * blk : (h + 1) * blk], 0), low_in, 0, 0)
        grad[h] = contract(left3(dnl[h * blk : (h + 1) * blk, :], 1), back_mid, 1, 0)

    @pl.loop(0, pl.cdiv(live, unroll))
    def _(i):
        done = []
        for j in range(unroll):
            s = i * unroll + j
            keep = (s < live).astype(f32)
            m = mb_ref[s]
            up = contract(left3(upw[s] * keep, 0), split_x[m], 0, 0)
            dn = contract(left3(dnw[s] * keep, 1), split_g[m], 1, 0)
            done.append((hb_ref[s], up, dn))
        for h, up, dn in done:
            pre[h] += up
            grad[h] += dn

    scale = 0.7978845608028654
    for h in range(blocks):
        v = pre[h]
        th = jnp.tanh(scale * (v + 0.044715 * (v * v * v)))
        hidden = 0.5 * v * (1.0 + th)
        slope = 0.5 * (1.0 + th) + 0.5 * v * (1.0 - th * th) * (scale * (1.0 + 3 * 0.044715 * (v * v)))
        back = grad[h] * slope
        hd[0, h] = hidden
        hd[1, h] = back
        hs, bs = right3(hidden, 0), right3(back, 0)
        split_hd[0, h] = hs
        split_hd[1, h] = bs
        lm = contract(left3(dnl[h * blk : (h + 1) * blk, :], 0), hs, 0, 0)
        bi = contract(left3(upr[:, h * blk : (h + 1) * blk], 1), bs, 1, 0)
        if h == 0:
            low[0] = lm
            low[1] = bi
        else:
            low[0] += lm
            low[1] += bi

    @pl.loop(0, pl.cdiv(live, unroll))
    def _(i):
        done = []
        for j in range(unroll):
            s = i * unroll + j
            keep = (s < live).astype(f32)
            h = hb_ref[s]
            dn = contract(left3(dnw[s] * keep, 0), split_hd[0, h], 0, 0)
            up = contract(left3(upw[s] * keep, 1), split_hd[1, h], 1, 0)
            done.append((mb_ref[s], dn, up))
        for m, dn, up in done:
            terms[m // bps, 0, m % bps] += dn
            terms[m // bps, 1, m % bps] += up


def grads_kernel(
    dp, unroll, mb_ref, hb_ref, live_ref,
    full, peer_g, peer_x, hd, peer_hd,
    peer_own, red, peer_red, low, peer_low, summed, upl, dnr,
    res, ing, upg, dng, uplg, uprg, dnlg, dnrg,
):
    slots, rows, blk = upg.shape
    bps = full.shape[2]
    blocks = hd.shape[1]
    d, t = lax.axis_index("dp"), lax.axis_index("tensor")
    live = live_ref[0]
    mine = pl.ds(pl.multiple_of(d * rows, rows), rows)
    peers = range(dp - 1)

    def cat(first, rest):
        return jnp.concatenate([first] + rest, axis=1)

    @pl.loop(0, slots // unroll)
    def _(i):
        for j in range(unroll):
            s = i * unroll + j
            keep = (s < live).astype(f32)
            m, h = mb_ref[s], hb_ref[s]
            q, r = m // bps, m % bps
            x = cat(full[q, 0, r, mine, :], [peer_x[k, q, r] for k in peers])
            back = cat(hd[1, h], [peer_hd[k, 1, h] for k in peers])
            upg[s] = dot3(x, back, 1, 1) * keep
            hidden = cat(hd[0, h, mine, :], [peer_hd[k, 0, h, mine, :] for k in peers])
            g = cat(full[q, 1, r], [peer_g[k, q, r] for k in peers])
            dng[s] = dot3(hidden, g, 1, 1) * keep

    for j in range(bps):
        span = slice(j * blk, (j + 1) * blk)
        res[:, span] = (summed[0, j] + dot3(dnr[:, span], low[0], 0, 0)).T
        ing[:, span] = (summed[1, j] + dot3(upl[span, :], low[1], 1, 0)).T
    back_in = right3(cat(low[1], [peer_low[k, 1] for k in peers]), 1)
    n = uplg.shape[0]
    step = min(n, blk)
    for j in range(n // step):
        at = d * n + j * step
        q = at // blk
        inner = pl.ds(pl.multiple_of(at % blk, step), step)
        x = cat(full[t, 0, q, inner, :], [peer_own[k, q, inner, :] for k in peers])
        uplg[j * step : (j + 1) * step, :] = contract(left3(x, 1), back_in, 1, 1)
    n = uprg.shape[0]
    span = pl.ds(pl.multiple_of(d * n, n), n)
    left_in = left3(cat(red[0, span, :], [peer_red[k, 0, span, :] for k in peers]), 1)
    left_mid = left3(cat(low[0, span, :], [peer_low[k, 0, span, :] for k in peers]), 1)
    for h in range(blocks):
        back = cat(hd[1, h], [peer_hd[k, 1, h] for k in peers])
        uprg[:, h * blk : (h + 1) * blk] = contract(left_in, right3(back, 1), 1, 1)
    for j in range(bps):
        g = cat(full[t, 1, j], [peer_g[k, t, j] for k in peers])
        dnrg[:, j * blk : (j + 1) * blk] = contract(left_mid, right3(g, 1), 1, 1)
    back_mid = right3(cat(red[1], [peer_red[k, 1] for k in peers]), 1)
    n = dnlg.shape[0]
    step = min(n, blk)
    for j in range(n // step):
        at = d * n + j * step
        h = at // blk
        inner = pl.ds(pl.multiple_of(at % blk, step), step)
        hidden = cat(hd[0, h, inner, :], [peer_hd[k, 0, h, inner, :] for k in peers])
        dnlg[j * step : (j + 1) * step, :] = contract(left3(hidden, 1), back_mid, 1, 1)


def shards(
    dp, T,
    inputs, out_grad, up_weight, down_weight, up_left, up_right, down_left, down_right,
    model_block, hidden_block, live_slots,
):
    tokens, feats = inputs.shape
    slots, blk = up_weight.shape[0], up_weight.shape[1]
    width = up_right.shape[1]
    rank = up_left.shape[1]
    blocks = width // blk
    bps = feats // blk
    A = T // 4
    peers = dp - 1
    unroll = 4 if slots % 4 == 0 else 1
    DMA = pltpu.SemaphoreType.DMA
    sds = lambda *shape: jax.ShapeDtypeStruct(shape, f32)
    steps = 2 * A - 1
    sends = 4 + 2 + 2 + 2 * 3 * (steps - 1) + 2 * steps + peers * (2 * steps + 2 * steps + 2) + 2 * (T - 1)
    rows = max(8, rank // T)
    limit = 60 << 20
    full, peer_g, peer_own, red, peer_red = pl.pallas_call(
        functools.partial(gather_kernel, dp, T),
        out_shape=(
            sds(T, 2, bps, blk, tokens),
            sds(peers, T, bps, blk, tokens),
            sds(peers, bps, blk, tokens),
            sds(2, rank, tokens),
            sds(peers, 2, rank, tokens),
        ),
        in_specs=[VM] * 4,
        out_specs=[VM] * 5,
        scratch_shapes=[
            pltpu.VMEM((bps, blk, tokens), f32),
            pltpu.VMEM((bps, blk, tokens), f32),
            pltpu.VMEM((2, rank, tokens), f32),
            pltpu.VMEM((T, 2, rows, tokens), f32),
            DMA((sends,)), DMA((T, 2)), DMA((peers, T)), DMA((peers,)),
            DMA((T,)), DMA((T,)), DMA((peers,)),
        ],
        compiler_params=pltpu.CompilerParams(collective_id=0, has_side_effects=True, vmem_limit_bytes=limit),
    )(inputs, out_grad, up_left, down_right)
    terms, low, hd = pl.pallas_call(
        functools.partial(layer_kernel, unroll),
        out_shape=(
            sds(T, 2, bps, blk, tokens),
            sds(2, rank, tokens),
            sds(2, blocks, blk, tokens),
        ),
        in_specs=[SM] * 3 + [VM] * 6,
        out_specs=[VM] * 3,
        scratch_shapes=[
            pltpu.VMEM((T * bps, 3 * blk, tokens), jnp.bfloat16),
            pltpu.VMEM((T * bps, 3 * blk, tokens), jnp.bfloat16),
            pltpu.VMEM((2, blocks, 3 * blk, tokens), jnp.bfloat16),
            pltpu.VMEM((blocks, blk, tokens), f32),
            pltpu.VMEM((blocks, blk, tokens), f32),
        ],
        compiler_params=pltpu.CompilerParams(vmem_limit_bytes=limit),
    )(model_block, hidden_block, live_slots, full, red, up_weight, down_weight, up_right, down_left)
    sends = 2 * A + A + (A - 1) + peers * (3 + 4 * A) + 2 * (T - 1)
    summed, low_total, peer_hd, peer_low, peer_x = pl.pallas_call(
        functools.partial(scatter_kernel, dp, T),
        out_shape=(
            sds(2, bps, blk, tokens),
            sds(2, rank, tokens),
            sds(peers, 2, blocks, blk, tokens),
            sds(peers, 2, rank, tokens),
            sds(peers, T, bps, blk // dp, tokens),
        ),
        in_specs=[VM] * 4,
        out_specs=[VM] * 5,
        scratch_shapes=[
            pltpu.VMEM((2 * A, 2, bps, blk, tokens), f32),
            pltpu.VMEM((A, 2, bps, blk, tokens), f32),
            pltpu.VMEM((A, 2, bps, blk, tokens), f32),
            pltpu.VMEM((A, 2, bps, blk, tokens), f32),
            pltpu.VMEM((A, 2, bps, blk, tokens), f32),
            pltpu.VMEM((T, 2, rows, tokens), f32),
            DMA((sends,)), DMA((2 * A,)), DMA((A,)), DMA((A,)), DMA((peers, 2)), DMA((peers, T)),
            DMA((T,)), DMA((T,)), DMA((peers,)),
        ],
        compiler_params=pltpu.CompilerParams(collective_id=1, has_side_effects=True, vmem_limit_bytes=limit),
    )(terms, low, hd, full)
    res, ing, upg, dng, uplg, uprg, dnlg, dnrg = pl.pallas_call(
        functools.partial(grads_kernel, dp, unroll),
        out_shape=(
            sds(tokens, feats),
            sds(tokens, feats),
            sds(slots, blk // dp, blk),
            sds(slots, blk // dp, blk),
            sds(feats // dp, rank),
            sds(rank // dp, width),
            sds(width // dp, rank),
            sds(rank // dp, feats),
        ),
        in_specs=[SM] * 3 + [VM] * 13,
        out_specs=[VM] * 8,
        compiler_params=pltpu.CompilerParams(vmem_limit_bytes=limit),
    )(
        model_block, hidden_block, live_slots,
        full, peer_g, peer_x, hd, peer_hd,
        peer_own, red, peer_red, low_total, peer_low, summed, up_left, down_right,
    )
    return res, ing, upg, dng, uplg, uprg, dnlg, dnrg


def solution(mesh):
    return jax.shard_map(
        functools.partial(shards, mesh.shape["dp"], mesh.shape["tensor"]),
        mesh=mesh,
        in_specs=(
            P("dp", "tensor"),
            P("dp", "tensor"),
            P("tensor", None, None),
            P("tensor", None, None),
            P("tensor", None),
            P(None, "tensor"),
            P("tensor", None),
            P(None, "tensor"),
            P("tensor"),
            P("tensor"),
            P("tensor"),
        ),
        out_specs=(
            P("dp", "tensor"),
            P("dp", "tensor"),
            P("tensor", "dp", None),
            P("tensor", "dp", None),
            P(("tensor", "dp"), None),
            P("dp", "tensor"),
            P(("tensor", "dp"), None),
            P("dp", "tensor"),
        ),
        check_vma=False,
    )
```

```python
import functools

import jax
import jax.numpy as jnp
from jax import lax
from jax.experimental import pallas as pl
from jax.experimental.pallas import tpu as pltpu
from jax.sharding import PartitionSpec as P

MESH = pl.DeviceIdType.MESH
VM = pl.BlockSpec(memory_space=pltpu.VMEM)
SM = pl.BlockSpec(memory_space=pltpu.SMEM)
f32 = jnp.float32


def halves(v):
    hi = v.astype(jnp.bfloat16)
    lo = (v - hi.astype(f32)).astype(jnp.bfloat16)
    return hi, lo


def left3(v, axis):
    hi, lo = halves(v)
    return jnp.concatenate([hi, hi, lo], axis=axis)


def right3(v, axis):
    hi, lo = halves(v)
    return jnp.concatenate([hi, lo, hi], axis=axis)


def contract(a, b, da, db):
    return lax.dot_general(a, b, (((da,), (db,)), ((), ())), preferred_element_type=f32)


def dot3(a, b, da, db):
    return contract(left3(a, da), right3(b, db), da, db)


def flip(a, k, size):
    out, bit = 0, 1
    while bit < size:
        out = out + (((a // bit) % 2 + (k // bit) % 2) % 2) * bit
        bit *= 2
    return out


class Copies:
    def __init__(self, sems):
        self.sems, self.count, self.made = sems, 0, []

    def send(self, src, dst, recv, where, cond=None):
        sem = self.sems.at[self.count]
        self.count += 1
        copy = pltpu.make_async_remote_copy(
            src_ref=src, dst_ref=dst, send_sem=sem, recv_sem=recv, device_id=where, device_id_type=MESH
        )
        if cond is None:
            copy.start()
        else:
            pl.when(cond)(copy.start)
        self.made.append((copy, cond))

    def drain(self):
        for copy, cond in self.made:
            if cond is None:
                copy.wait_send()
            else:
                pl.when(cond)(copy.wait_send)


def arrived(ref, recv, where, cond=None):
    copy = pltpu.make_async_remote_copy(
        src_ref=ref, dst_ref=ref, send_sem=recv, recv_sem=recv, device_id=where, device_id_type=MESH
    )
    if cond is None:
        copy.wait_recv()
    else:
        pl.when(cond)(copy.wait_recv)


def line_steps(a, A):
    out = [(a, 0, None)]
    for k in range(1, A):
        out.append(((a + A - k) % A, -1, a >= k))
        out.append(((a + k) % A, 1, a + k < A))
    return out


def greet(d, t, dp, T):
    barrier = pltpu.get_barrier_semaphore()
    for k in range(1, T):
        pl.semaphore_signal(barrier, inc=1, device_id=(d, lax.rem(t + k, T)), device_id_type=MESH)
    for k in range(1, dp):
        pl.semaphore_signal(barrier, inc=1, device_id=(lax.rem(d + k, dp), t), device_id_type=MESH)
    pl.semaphore_wait(barrier, T - 1 + dp - 1)


class Total:
    def __init__(self, out, d, t, T, part, inbox, copies, in_sem, out_sem):
        self.out, self.d, self.t, self.T, self.part, self.inbox = out, d, t, T, part, inbox
        self.copies, self.in_sem, self.out_sem = copies, in_sem, out_sem
        rank = part.shape[1]
        self.rows = max(8, rank // T)
        self.count = rank // self.rows

    def cond(self, j):
        return None if self.count >= self.T else j < self.count

    def piece(self, ref, j):
        return ref.at[:, pl.ds(pl.multiple_of(j * self.rows, self.rows), self.rows), :]

    def begin(self):
        for k in range(1, self.T):
            j = lax.rem(self.t + k, self.T)
            cond = self.cond(j)
            at = j if cond is None else lax.rem(j, self.count)
            self.copies.send(
                self.piece(self.part, at), self.inbox.at[self.T - k], self.in_sem.at[self.T - k], (self.d, j), cond
            )

    def reduce(self):
        cond = self.cond(self.t)
        at = self.t if cond is None else lax.rem(self.t, self.count)

        def work():
            span = pl.ds(pl.multiple_of(at * self.rows, self.rows), self.rows)
            total = self.part[:, span, :]
            for k in range(1, self.T):
                arrived(self.inbox.at[k], self.in_sem.at[k], (self.d, self.t))
                total = total + self.inbox[k]
            self.out[:, span, :] = total

        if cond is None:
            work()
        else:
            pl.when(cond)(work)
        for k in range(1, self.T):
            j = lax.rem(self.t + k, self.T)
            self.copies.send(
                self.piece(self.out, at), self.piece(self.out, at), self.out_sem.at[self.T - k], (self.d, j), cond
            )

    def finish(self):
        for k in range(1, self.T):
            j = lax.rem(self.t + k, self.T)
            cond = self.cond(j)
            at = j if cond is None else lax.rem(j, self.count)
            wait = functools.partial(arrived, self.piece(self.out, at), self.out_sem.at[k], (self.d, j))
            if cond is None:
                wait()
            else:
                pl.when(cond)(wait)


def gather_kernel(
    dp, T, inp_ref, og_ref, upl_ref, dnr_ref,
    full, peer_g, peer_own, red, peer_red,
    x_ref, g_ref, part, inbox, send_sem, full_sem, pg_sem, po_sem, in_sem, out_sem, pr_sem,
):
    d, t = lax.axis_index("dp"), lax.axis_index("tensor")
    c, b, a = t % 2, (t // 2) % 2, t // 4
    A = T // 4
    bps, blk = x_ref.shape[0], x_ref.shape[1]
    for j in range(bps):
        x_ref[j] = inp_ref[:, j * blk : (j + 1) * blk].T
        g_ref[j] = og_ref[:, j * blk : (j + 1) * blk].T
    core, side = (d, a * 4 + b * 2 + 1 - c), (d, a * 4 + (1 - b) * 2 + c)
    before, after = (d, (t + T - 4) % T), (d, (t + 4) % T)
    copies = Copies(send_sem)
    greet(d, t, dp, T)

    def to_peers(src_g, s, cond=None):
        for k in range(dp - 1):
            copies.send(src_g, peer_g.at[k, s], pg_sem.at[k, s], (lax.rem(d + k + 1, dp), t), cond)

    def two(src_x, src_g, s, where, cond=None):
        copies.send(src_x, full.at[s, 0], full_sem.at[s, 0], where, cond)
        copies.send(src_g, full.at[s, 1], full_sem.at[s, 1], where, cond)

    def got(s, where, cond=None):
        arrived(full.at[s, 0], full_sem.at[s, 0], where, cond)
        arrived(full.at[s, 1], full_sem.at[s, 1], where, cond)

    two(x_ref, g_ref, t, before, a >= 1)
    two(x_ref, g_ref, t, after, a + 1 < A)
    two(x_ref, g_ref, t, side)
    to_peers(g_ref, t)
    two(x_ref, g_ref, t, core)
    feats = bps * blk
    part[0] = dot3(upl_ref[...], x_ref[...].reshape(feats, x_ref.shape[2]), 0, 0)
    part[1] = dot3(dnr_ref[...], g_ref[...].reshape(feats, x_ref.shape[2]), 1, 0)
    total = Total(red, d, t, T, part, inbox, copies, in_sem, out_sem)
    total.begin()
    full[t, 0] = x_ref[...]
    full[t, 1] = g_ref[...]
    mine = []
    for row, way, here in line_steps(a, A):
        s = row * 4 + b * 2 + c
        if way != 0:
            got(s, side, here)
            onward = (here & (a + 1 < A)) if way < 0 else (here & (a >= 1))
            two(full.at[s, 0], full.at[s, 1], s, after if way < 0 else before, onward)
            two(full.at[s, 0], full.at[s, 1], s, side, here)
            to_peers(full.at[s, 1], s, here)
            two(full.at[s, 0], full.at[s, 1], s, core, here)
        mine.append((s, here))
        s = row * 4 + (1 - b) * 2 + c
        got(s, side, here)
        to_peers(full.at[s, 1], s, here)
        two(full.at[s, 0], full.at[s, 1], s, core, here)
        mine.append((s, here))
        if way == 0:
            total.reduce()
    total.finish()
    for k in range(dp - 1):
        copies.send(red, peer_red.at[k], pr_sem.at[k], (lax.rem(d + k + 1, dp), t))
        copies.send(x_ref, peer_own.at[k], po_sem.at[k], (lax.rem(d + k + 1, dp), t))
    for s, here in mine:
        for k in range(dp - 1):
            arrived(peer_g.at[k, s], pg_sem.at[k, s], core, here)
            copies.send(peer_g.at[k, s], peer_g.at[k, s], pg_sem.at[k, s], core, here)
    for k in range(2 * A):
        s = k * 2 + 1 - c
        got(s, core)
        for p in range(dp - 1):
            arrived(peer_g.at[p, s], pg_sem.at[p, s], core)
    for k in range(dp - 1):
        arrived(peer_own.at[k], po_sem.at[k], core)
        arrived(peer_red.at[k], pr_sem.at[k], core)
    copies.drain()


def scatter_kernel(
    dp, T, unroll, mb_ref, hb_ref, live_ref, terms, low, hd, full, peer_g,
    summed, red, peer_hd, peer_red, peer_x, dng,
    core_box, stage, side_box, acc, line_box, inbox,
    send_sem, core_sem, side_sem, line_sem, hd_sem, px_sem, in_sem, out_sem, pr_sem,
):
    d, t = lax.axis_index("dp"), lax.axis_index("tensor")
    c, b, a = t % 2, (t // 2) % 2, t // 4
    A = T // 4
    core, side = (d, a * 4 + b * 2 + 1 - c), (d, a * 4 + (1 - b) * 2 + c)
    copies = Copies(send_sem)
    greet(d, t, dp, T)
    order = [flip(a, k, A) for k in range(A)][::-1]
    for far in (1, 0):
        for row in order:
            col = (1 - b) if far else b
            i = row * 2 + col
            copies.send(terms.at[i * 2 + 1 - c], core_box.at[i], core_sem.at[i], core)
    for k in range(dp - 1):
        for n in range(2):
            copies.send(hd.at[n], peer_hd.at[k, n], hd_sem.at[k, n], (lax.rem(d + k + 1, dp), t))
    total = Total(red, d, t, T, low, inbox, copies, in_sem, out_sem)
    total.begin()
    part_rows = peer_x.shape[3]
    for n in range(2 * A):
        for k in range(dp - 1):
            other = lax.rem(d + k + 1, dp)
            rows = pl.ds(pl.multiple_of(other * part_rows, part_rows), part_rows)
            s = n * 2 + c
            copies.send(full.at[s, 0, :, rows, :], peer_x.at[k, s], px_sem.at[k, s], (other, t))
    for row in order:
        i = row * 2 + 1 - b
        arrived(core_box.at[i], core_sem.at[i], core)
        stage[row] = terms[i * 2 + c] + core_box[i]
        copies.send(stage.at[row], side_box.at[row], side_sem.at[row], side)
    total.reduce()
    for n, row in enumerate(order):
        i = row * 2 + b
        k = A - 1 - n
        arrived(core_box.at[i], core_sem.at[i], core)
        arrived(side_box.at[row], side_sem.at[row], side)
        acc[row] = terms[i * 2 + c] + core_box[i] + side_box[row]
        if k > 0:
            copies.send(acc.at[row], line_box.at[k], line_sem.at[k], (d, row * 4 + b * 2 + c))
    total.finish()
    for k in range(dp - 1):
        copies.send(red, peer_red.at[k], pr_sem.at[k], (lax.rem(d + k + 1, dp), t))
    for k in range(dp - 1):
        arrived(peer_hd.at[k, 0], hd_sem.at[k, 0], core)
        arrived(peer_hd.at[k, 1], hd_sem.at[k, 1], core)
    slots, half, _ = dng.shape
    bps = full.shape[2]
    live = live_ref[0]
    mine = pl.ds(pl.multiple_of(d * half, half), half)

    @pl.loop(0, slots // unroll)
    def _(i):
        for j in range(unroll):
            s = i * unroll + j
            keep = (s < live).astype(f32)
            m, h = mb_ref[s], hb_ref[s]
            hidden = [hd[0, h, mine, :]] + [peer_hd[k, 0, h, mine, :] for k in range(dp - 1)]
            g = [full[m // bps, 1, m % bps]] + [peer_g[k, m // bps, m % bps] for k in range(dp - 1)]
            dng[s] = dot3(jnp.concatenate(hidden, axis=1), jnp.concatenate(g, axis=1), 1, 1) * keep

    result = acc[a]
    for k in range(1, A):
        arrived(line_box.at[k], line_sem.at[k], core)
        result = result + line_box[k]
    summed[...] = result
    for n in range(2 * A):
        for k in range(dp - 1):
            s = n * 2 + c
            arrived(peer_x.at[k, s], px_sem.at[k, s], core)
            copies.send(peer_x.at[k, s], peer_x.at[k, s], px_sem.at[k, s], core)
    for k in range(dp - 1):
        for n in range(2 * A):
            s = n * 2 + 1 - c
            arrived(peer_x.at[k, s], px_sem.at[k, s], core)
        arrived(peer_red.at[k], pr_sem.at[k], core)
    copies.drain()


def layer_kernel(
    unroll, mb_ref, hb_ref, live_ref, full, red, upw, dnw, upr, dnl,
    terms, low, hd,
    split_x, split_g, split_hd, pre, grad,
):
    slots, blk = upw.shape[0], upw.shape[1]
    bps, tokens = full.shape[2], full.shape[4]
    blocks = hd.shape[1]
    live = live_ref[0]

    @pl.loop(0, full.shape[0])
    def _(s):
        for j in range(bps):
            split_x[s * bps + j] = right3(full[s, 0, j], 0)
            split_g[s * bps + j] = right3(full[s, 1, j], 0)
            terms[s, 0, j] = jnp.zeros((blk, tokens), f32)
            terms[s, 1, j] = jnp.zeros((blk, tokens), f32)

    low_in, back_mid = right3(red[0], 0), right3(red[1], 0)
    for h in range(blocks):
        pre[h] = contract(left3(upr[:, h * blk : (h + 1) * blk], 0), low_in, 0, 0)
        grad[h] = contract(left3(dnl[h * blk : (h + 1) * blk, :], 1), back_mid, 1, 0)

    @pl.loop(0, pl.cdiv(live, unroll))
    def _(i):
        done = []
        for j in range(unroll):
            s = i * unroll + j
            keep = (s < live).astype(f32)
            m = mb_ref[s]
            up = contract(left3(upw[s] * keep, 0), split_x[m], 0, 0)
            dn = contract(left3(dnw[s] * keep, 1), split_g[m], 1, 0)
            done.append((hb_ref[s], up, dn))
        for h, up, dn in done:
            pre[h] += up
            grad[h] += dn

    scale = 0.7978845608028654
    for h in range(blocks):
        v = pre[h]
        th = jnp.tanh(scale * (v + 0.044715 * (v * v * v)))
        hidden = 0.5 * v * (1.0 + th)
        slope = 0.5 * (1.0 + th) + 0.5 * v * (1.0 - th * th) * (scale * (1.0 + 3 * 0.044715 * (v * v)))
        back = grad[h] * slope
        hd[0, h] = hidden
        hd[1, h] = back
        hs, bs = right3(hidden, 0), right3(back, 0)
        split_hd[0, h] = hs
        split_hd[1, h] = bs
        lm = contract(left3(dnl[h * blk : (h + 1) * blk, :], 0), hs, 0, 0)
        bi = contract(left3(upr[:, h * blk : (h + 1) * blk], 1), bs, 1, 0)
        if h == 0:
            low[0] = lm
            low[1] = bi
        else:
            low[0] += lm
            low[1] += bi

    @pl.loop(0, pl.cdiv(live, unroll))
    def _(i):
        done = []
        for j in range(unroll):
            s = i * unroll + j
            keep = (s < live).astype(f32)
            h = hb_ref[s]
            dn = contract(left3(dnw[s] * keep, 0), split_hd[0, h], 0, 0)
            up = contract(left3(upw[s] * keep, 1), split_hd[1, h], 1, 0)
            done.append((mb_ref[s], dn, up))
        for m, dn, up in done:
            terms[m // bps, 0, m % bps] += dn
            terms[m // bps, 1, m % bps] += up


def grads_kernel(
    dp, unroll, mb_ref, hb_ref, live_ref,
    full, peer_g, peer_x, hd, peer_hd,
    peer_own, red, peer_red, low, peer_low, summed, upl, dnr,
    res, ing, upg, uplg, uprg, dnlg, dnrg,
):
    slots, rows, blk = upg.shape
    bps = full.shape[2]
    blocks = hd.shape[1]
    d, t = lax.axis_index("dp"), lax.axis_index("tensor")
    live = live_ref[0]
    mine = pl.ds(pl.multiple_of(d * rows, rows), rows)
    peers = range(dp - 1)

    def cat(first, rest):
        return jnp.concatenate([first] + rest, axis=1)

    @pl.loop(0, slots // unroll)
    def _(i):
        for j in range(unroll):
            s = i * unroll + j
            keep = (s < live).astype(f32)
            m, h = mb_ref[s], hb_ref[s]
            q, r = m // bps, m % bps
            x = cat(full[q, 0, r, mine, :], [peer_x[k, q, r] for k in peers])
            back = cat(hd[1, h], [peer_hd[k, 1, h] for k in peers])
            upg[s] = dot3(x, back, 1, 1) * keep

    for j in range(bps):
        span = slice(j * blk, (j + 1) * blk)
        res[:, span] = (summed[0, j] + dot3(dnr[:, span], low[0], 0, 0)).T
        ing[:, span] = (summed[1, j] + dot3(upl[span, :], low[1], 1, 0)).T
    back_in = right3(cat(low[1], [peer_low[k, 1] for k in peers]), 1)
    n = uplg.shape[0]
    step = min(n, blk)
    for j in range(n // step):
        at = d * n + j * step
        q = at // blk
        inner = pl.ds(pl.multiple_of(at % blk, step), step)
        x = cat(full[t, 0, q, inner, :], [peer_own[k, q, inner, :] for k in peers])
        uplg[j * step : (j + 1) * step, :] = contract(left3(x, 1), back_in, 1, 1)
    n = uprg.shape[0]
    span = pl.ds(pl.multiple_of(d * n, n), n)
    left_in = left3(cat(red[0, span, :], [peer_red[k, 0, span, :] for k in peers]), 1)
    left_mid = left3(cat(low[0, span, :], [peer_low[k, 0, span, :] for k in peers]), 1)
    for h in range(blocks):
        back = cat(hd[1, h], [peer_hd[k, 1, h] for k in peers])
        uprg[:, h * blk : (h + 1) * blk] = contract(left_in, right3(back, 1), 1, 1)
    for j in range(bps):
        g = cat(full[t, 1, j], [peer_g[k, t, j] for k in peers])
        dnrg[:, j * blk : (j + 1) * blk] = contract(left_mid, right3(g, 1), 1, 1)
    back_mid = right3(cat(red[1], [peer_red[k, 1] for k in peers]), 1)
    n = dnlg.shape[0]
    step = min(n, blk)
    for j in range(n // step):
        at = d * n + j * step
        h = at // blk
        inner = pl.ds(pl.multiple_of(at % blk, step), step)
        hidden = cat(hd[0, h, inner, :], [peer_hd[k, 0, h, inner, :] for k in peers])
        dnlg[j * step : (j + 1) * step, :] = contract(left3(hidden, 1), back_mid, 1, 1)


def shards(
    dp, T,
    inputs, out_grad, up_weight, down_weight, up_left, up_right, down_left, down_right,
    model_block, hidden_block, live_slots,
):
    tokens, feats = inputs.shape
    slots, blk = up_weight.shape[0], up_weight.shape[1]
    width = up_right.shape[1]
    rank = up_left.shape[1]
    blocks = width // blk
    bps = feats // blk
    A = T // 4
    peers = dp - 1
    unroll = 4 if slots % 4 == 0 else 1
    DMA = pltpu.SemaphoreType.DMA
    sds = lambda *shape: jax.ShapeDtypeStruct(shape, f32)
    steps = 2 * A - 1
    sends = 4 + 2 + 2 + 2 * 3 * (steps - 1) + 2 * steps + peers * (2 * steps + 2 * steps + 2) + 2 * (T - 1)
    rows = max(8, rank // T)
    limit = 60 << 20
    full, peer_g, peer_own, red, peer_red = pl.pallas_call(
        functools.partial(gather_kernel, dp, T),
        out_shape=(
            sds(T, 2, bps, blk, tokens),
            sds(peers, T, bps, blk, tokens),
            sds(peers, bps, blk, tokens),
            sds(2, rank, tokens),
            sds(peers, 2, rank, tokens),
        ),
        in_specs=[VM] * 4,
        out_specs=[VM] * 5,
        scratch_shapes=[
            pltpu.VMEM((bps, blk, tokens), f32),
            pltpu.VMEM((bps, blk, tokens), f32),
            pltpu.VMEM((2, rank, tokens), f32),
            pltpu.VMEM((T, 2, rows, tokens), f32),
            DMA((sends,)), DMA((T, 2)), DMA((peers, T)), DMA((peers,)),
            DMA((T,)), DMA((T,)), DMA((peers,)),
        ],
        compiler_params=pltpu.CompilerParams(collective_id=0, has_side_effects=True, vmem_limit_bytes=limit),
    )(inputs, out_grad, up_left, down_right)
    terms, low, hd = pl.pallas_call(
        functools.partial(layer_kernel, unroll),
        out_shape=(
            sds(T, 2, bps, blk, tokens),
            sds(2, rank, tokens),
            sds(2, blocks, blk, tokens),
        ),
        in_specs=[SM] * 3 + [VM] * 6,
        out_specs=[VM] * 3,
        scratch_shapes=[
            pltpu.VMEM((T * bps, 3 * blk, tokens), jnp.bfloat16),
            pltpu.VMEM((T * bps, 3 * blk, tokens), jnp.bfloat16),
            pltpu.VMEM((2, blocks, 3 * blk, tokens), jnp.bfloat16),
            pltpu.VMEM((blocks, blk, tokens), f32),
            pltpu.VMEM((blocks, blk, tokens), f32),
        ],
        compiler_params=pltpu.CompilerParams(vmem_limit_bytes=limit),
    )(model_block, hidden_block, live_slots, full, red, up_weight, down_weight, up_right, down_left)
    sends = 2 * A + A + (A - 1) + peers * (3 + 4 * A) + 2 * (T - 1)
    summed, low_total, peer_hd, peer_low, peer_x, dng = pl.pallas_call(
        functools.partial(scatter_kernel, dp, T, unroll),
        out_shape=(
            sds(2, bps, blk, tokens),
            sds(2, rank, tokens),
            sds(peers, 2, blocks, blk, tokens),
            sds(peers, 2, rank, tokens),
            sds(peers, T, bps, blk // dp, tokens),
            sds(slots, blk // dp, blk),
        ),
        in_specs=[SM] * 3 + [VM] * 5,
        out_specs=[VM] * 6,
        scratch_shapes=[
            pltpu.VMEM((2 * A, 2, bps, blk, tokens), f32),
            pltpu.VMEM((A, 2, bps, blk, tokens), f32),
            pltpu.VMEM((A, 2, bps, blk, tokens), f32),
            pltpu.VMEM((A, 2, bps, blk, tokens), f32),
            pltpu.VMEM((A, 2, bps, blk, tokens), f32),
            pltpu.VMEM((T, 2, rows, tokens), f32),
            DMA((sends,)), DMA((2 * A,)), DMA((A,)), DMA((A,)), DMA((peers, 2)), DMA((peers, T)),
            DMA((T,)), DMA((T,)), DMA((peers,)),
        ],
        compiler_params=pltpu.CompilerParams(collective_id=1, has_side_effects=True, vmem_limit_bytes=limit),
    )(model_block, hidden_block, live_slots, terms, low, hd, full, peer_g)
    res, ing, upg, uplg, uprg, dnlg, dnrg = pl.pallas_call(
        functools.partial(grads_kernel, dp, unroll),
        out_shape=(
            sds(tokens, feats),
            sds(tokens, feats),
            sds(slots, blk // dp, blk),
            sds(feats // dp, rank),
            sds(rank // dp, width),
            sds(width // dp, rank),
            sds(rank // dp, feats),
        ),
        in_specs=[SM] * 3 + [VM] * 13,
        out_specs=[VM] * 7,
        compiler_params=pltpu.CompilerParams(vmem_limit_bytes=limit),
    )(
        model_block, hidden_block, live_slots,
        full, peer_g, peer_x, hd, peer_hd,
        peer_own, red, peer_red, low_total, peer_low, summed, up_left, down_right,
    )
    return res, ing, upg, dng, uplg, uprg, dnlg, dnrg


def solution(mesh):
    return jax.shard_map(
        functools.partial(shards, mesh.shape["dp"], mesh.shape["tensor"]),
        mesh=mesh,
        in_specs=(
            P("dp", "tensor"),
            P("dp", "tensor"),
            P("tensor", None, None),
            P("tensor", None, None),
            P("tensor", None),
            P(None, "tensor"),
            P("tensor", None),
            P(None, "tensor"),
            P("tensor"),
            P("tensor"),
            P("tensor"),
        ),
        out_specs=(
            P("dp", "tensor"),
            P("dp", "tensor"),
            P("tensor", "dp", None),
            P("tensor", "dp", None),
            P(("tensor", "dp"), None),
            P("dp", "tensor"),
            P(("tensor", "dp"), None),
            P("dp", "tensor"),
        ),
        check_vma=False,
    )
```
